32 devices in a mesh: fsdp: 8 (over y, x, core), tensor: 4 (over z).
Axes of the slice: x: 2, y: 2, z: 4, core: 2. Of those that a mesh axis runs over, the one named last changes fastest.
Arguments:
- tokens: float32 [3152, 768], P('fsdp'), may hold values from -6 to 6
- cotangent: float32 [3152, 768], P('fsdp'), may hold values from -6 to 6
- expert_ids: int32 [3152, 2], P('fsdp'), may hold values from 0 to 15, all different within a row; in each aligned block of 394 rows (0 to 393, 394 to 787, ...) at most 96 rows name the same one
- image_counts: int32 [8], P('fsdp'), may hold values from 1 to 2, as said below
- w_attn: bfloat16 [2, 768, 4, 768], P(None, 'fsdp', None, 'tensor')
- norm_gain: bfloat16 [2, 2, 768], P(None, None, 'fsdp'), may hold values from 0.5 to 1.5
- norm_bias: bfloat16 [2, 2, 768], P(None, None, 'fsdp'), may hold values from -1.75 to 1.75
- mlp_in: bfloat16 [768, 3072], P('fsdp', 'tensor'), may hold values from -0.21875 to 0.21875
- mlp_out: bfloat16 [768, 3072], P('fsdp', 'tensor'), may hold values from -0.109375 to 0.109375
- router: bfloat16 [768, 16], P('fsdp'), may hold values from -0.4375 to 0.4375
- exp_in: bfloat16 [16, 768, 3072], P(None, 'fsdp', 'tensor'), may hold values from -0.21875 to 0.21875
- exp_out: bfloat16 [16, 768, 3072], P(None, 'fsdp', 'tensor'), may hold values from -0.625 to 0.625
Outputs:
- output: float32 [3152, 768], P('fsdp')
- grad_tokens: float32 [3152, 768], P('fsdp')
- grad_attn: float32 [2, 768, 4, 768], P(None, 'fsdp', None, 'tensor')
- grad_gain: float32 [2, 2, 768], P(None, None, 'fsdp')
- grad_bias: float32 [2, 2, 768], P(None, None, 'fsdp')
- grad_mlp_in: float32 [768, 3072], P('fsdp', 'tensor')
- grad_mlp_out: float32 [768, 3072], P('fsdp', 'tensor')
- grad_router: float32 [768, 16], P('fsdp')
- grad_exp_in: float32 [16, 768, 3072], P(None, 'fsdp', 'tensor')
- grad_exp_out: float32 [16, 768, 3072], P(None, 'fsdp', 'tensor')
The draws below stay inside these ranges and needn't reach their ends.
Inputs may be any that keep to these rules, and one draw needn't show every extreme that they name: `expert_ids`: within the rows of one index of fsdp no expert is named by more than 96 rows; the two experts of a row differ. `image_counts`: some index of fsdp has all 2 images in use.
All inputs are finite; a program needn't handle non-finite values.
Results may differ from the reference program's by a relative error of at most 0.033.
Values may be sent and summed in bfloat16 or wider, within the bound.
A program may use at most 256 MiB of HBM per device.

```python
import math
import jax
import jax.numpy as jnp
import numpy as np
from jax import lax

D = 768
HD = 64
FF = 3072
E = 16
SEQ = 197
IMG_DEV = 2
CAP = 96
TOKENS = 3152
N_FSDP = 8


def draw_image_counts(key, part):
    counts = jax.random.randint(key, (N_FSDP,), 1, IMG_DEV + 1)
    fullest = jax.random.randint(jax.random.fold_in(key, 3), (), 0, N_FSDP)
    return jnp.where(jnp.arange(N_FSDP) == fullest, IMG_DEV, counts).astype(jnp.int32)


def draw_w_attn(key, part):
    base = jax.random.normal(key, (2, D, 4, D), jnp.float32) * D ** (-0.5)
    boost = jnp.array([1.0, 1.0, 1.0, 4.0], jnp.float32)[None, None, :, None]
    drawn = base * boost
    return drawn.astype(jnp.bfloat16)


def block_levels(rng, shape, split, low, top_value):
    factor_of = 1.0
    for dim, parts in split:
        draws = jax.random.uniform(jax.random.fold_in(jax.random.fold_in(rng, 6), dim), (parts,), jnp.float32, low / len(split), top_value / len(split))
        factor_of = factor_of * jnp.repeat(jnp.exp(draws), shape[dim] // parts).reshape((-1,) + (1,) * (len(shape) - 1 - dim))
    return factor_of


def routed_block(own_key, own, number, rows, count, top, most, skew):
    ranking = jax.random.permutation(own_key, count)
    packed, usual = load_shares(count, rows * top, most, skew, True), load_shares(count, rows * top, most, skew, False)
    places = jnp.arange(count)

    def named(tallies, turn):
        used = int((tallies > 0).sum())
        fixed = max(1, used // 4)
        shifted = fixed + (places - fixed + turn * (used - fixed)) % max(1, count - fixed)
        return jnp.zeros((count,), jnp.int32).at[ranking[jnp.where(places < fixed, places, shifted)]].set(jnp.asarray(tallies, jnp.int32))

    tallies = jnp.where(number % 4 == 0, named(packed, number // 4), named(usual, number - number // 4 - 1))
    mixed = jax.random.permutation(jax.random.fold_in(own, 3), count)
    source_of, sink = mixed[0:count // 2 * 2:2], mixed[1:count // 2 * 2:2]
    slack = jnp.minimum(tallies[source_of] - 1, most - tallies[sink]) // 2
    slack = jnp.where((source_of == ranking[0]) | (sink == ranking[0]) | (tallies[sink] == 0), 0, jnp.maximum(slack, 0))
    shifted = jax.random.randint(jax.random.fold_in(own, 4), (count // 2,), 0, 1 << 20) % (slack + 1)
    tallies = tallies.at[source_of].add(-shifted).at[sink].add(shifted)
    items = jnp.searchsorted(jnp.cumsum(tallies), jnp.arange(rows * top), side="right").astype(jnp.int32)
    listing = items.reshape(top, rows).T
    listing = listing[jax.random.permutation(jax.random.fold_in(own, 1), rows)]
    turn = jax.random.randint(jax.random.fold_in(own, 2), (rows, 1), 0, top)
    return jnp.take_along_axis(listing, (jnp.arange(top)[None, :] + turn) % top, axis=1)


def load_shares(count, total, limit, skew, full):
    portions = [(1 << 20) // math.isqrt(rank ** skew) + 1 for rank in range(1, count + 1)]
    largest = limit if full else min(limit, max(-(-total // count), total * portions[0] // sum(portions)))
    least = 1 if total - largest >= count - 1 else 0
    given, surplus = [largest] + [least] * (count - 1), total - largest - least * (count - 1)
    while surplus > 0:
        movable = [i for i in range(1, count) if given[i] < largest] or [i for i in range(1, count) if given[i] < limit]
        whole, budget = sum([portions[i] for i in movable]), surplus
        for i in movable:
            addition = min(limit - given[i], max(1, budget * portions[i] // whole), surplus)
            given[i] = given[i] + addition
            surplus = surplus - addition
    return np.array(given)


def bell_draw(key, dims, scale, limit, split=(), kind=jnp.bfloat16):
    factor_of = block_levels(key, dims, split, -0.22, 0.18) if split else 1.0
    values = jax.random.normal(key, dims, jnp.float32) * scale * factor_of
    return jnp.minimum(jnp.maximum(values, -limit), limit).astype(kind)


def setup_inputs(seed: int = 0) -> dict:
    seeds = jax.random.split(jax.random.key(seed), 13)
    tokens = bell_draw(seeds[0], (TOKENS, D), 1.0, 6.0, ((0, 8),), jnp.float32)
    cotangent = bell_draw(seeds[1], (TOKENS, D), 1.0, 6.0, ((0, 8),), jnp.float32)
    expert_ids_keys = jax.random.split(jax.random.fold_in(seeds[2], 1), TOKENS // (IMG_DEV * SEQ))
    expert_ids_turns = jax.random.permutation(jax.random.fold_in(seeds[2], 3), TOKENS // (IMG_DEV * SEQ))
    expert_ids = jax.vmap(lambda own, number: routed_block(jax.random.fold_in(seeds[2], 2), own, number, IMG_DEV * SEQ, E, 2, CAP, 1))(expert_ids_keys, expert_ids_turns).reshape((TOKENS, 2))
    image_counts = draw_image_counts(jax.random.fold_in(seeds[12], 71), 0)
    w_attn = draw_w_attn(jax.random.fold_in(seeds[12], 71), 0)
    norm_gain = jnp.clip(1.0 + 0.1 * jax.random.normal(seeds[5], (2, 2, D), jnp.float32), 0.5, 1.5).astype(jnp.bfloat16)
    norm_bias = bell_draw(seeds[6], (2, 2, D), 0.3, 1.75, ((2, 8),))
    mlp_in = bell_draw(seeds[7], (D, FF), D ** -0.5, 0.21875, ((0, 8), (1, 4)))
    mlp_out = bell_draw(seeds[8], (D, FF), FF ** -0.5, 0.109375, ((0, 8), (1, 4)))
    router = bell_draw(seeds[9], (D, E), (D // 4) ** -0.5, 0.4375, ((0, 8),))
    exp_in = bell_draw(seeds[10], (E, D, FF), D ** -0.5, 0.21875, ((1, 8), (2, 4)))
    exp_out = bell_draw(seeds[11], (E, D, FF), (FF // 36) ** -0.5, 0.625, ((1, 8), (2, 4)))
    return dict(tokens=tokens, cotangent=cotangent, expert_ids=expert_ids, image_counts=image_counts, w_attn=w_attn, norm_gain=norm_gain, norm_bias=norm_bias, mlp_in=mlp_in, mlp_out=mlp_out, router=router, exp_in=exp_in, exp_out=exp_out)


EPS = 1e-06
ROOT_HALF = 0.7071067811865476
INV_ROOT_TAU = 0.3989422804014327

def product(form, left, right):
    return jnp.einsum(form, left.astype(jnp.float32), right.astype(jnp.float32), precision=lax.Precision.HIGHEST)

def gelu_value(values):
    return values * 0.5 * (1.0 + lax.erf(values * ROOT_HALF))

def gelu_slope(values):
    return 0.5 * (1.0 + lax.erf(values * ROOT_HALF)) + values * jnp.exp(-0.5 * values * values) * INV_ROOT_TAU

def norm_forward(inputs, weight_gain, weight_bias):
    center = inputs - lax.optimization_barrier(jnp.mean(inputs, axis=-1, keepdims=True))
    inverse = lax.rsqrt(lax.optimization_barrier(jnp.mean(center * center, axis=-1, keepdims=True)) + EPS)
    normed = center * inverse
    return (normed * weight_gain + weight_bias, normed, inverse)

def norm_backward(upstream, normed, inverse, weight_gain):
    scaled = upstream * weight_gain
    result = inverse * (scaled - lax.optimization_barrier(jnp.mean(scaled, axis=-1, keepdims=True)) - normed * lax.optimization_barrier(jnp.mean(scaled * normed, axis=-1, keepdims=True)))
    return (result, lax.optimization_barrier(jnp.sum(upstream * normed, axis=0)), lax.optimization_barrier(jnp.sum(upstream, axis=0)))

def route_slots(expert_ids, live, experts, capacity):
    flat_ids = expert_ids.reshape(-1)
    flat_live = jnp.repeat(live, expert_ids.shape[1])
    onehot = (flat_ids[:, None] == jnp.arange(experts, dtype=jnp.int32)[None, :]).astype(jnp.int32) * flat_live[:, None]
    earlier = jnp.cumsum(onehot, axis=0) - onehot
    position = lax.optimization_barrier(jnp.sum(earlier * onehot, axis=1)).astype(jnp.int32)
    target = jnp.where(flat_live > 0, flat_ids * capacity + position, experts * capacity)
    return target.reshape(expert_ids.shape).astype(jnp.int32)

def attend_forward(normed_b, weights, images):
    total_rows = normed_b.shape[0]
    head_cols = weights.shape[2]
    scaling = HD ** (-0.5)
    shaped = (images, total_rows // images, head_cols // HD, HD)
    queries = product('rd,dc->rc', normed_b, weights[:, 0, :]).astype(jnp.bfloat16).reshape(shaped)
    keyed = product('rd,dc->rc', normed_b, weights[:, 1, :]).astype(jnp.bfloat16).reshape(shaped)
    valued = product('rd,dc->rc', normed_b, weights[:, 2, :]).astype(jnp.bfloat16).reshape(shaped)
    scores = product('ishd,ithd->ihst', queries, keyed) * scaling
    highest = lax.optimization_barrier(jnp.max(scores, axis=-1, keepdims=True))
    log_total = highest + jnp.log(lax.optimization_barrier(jnp.sum(jnp.exp(scores - highest), axis=-1, keepdims=True)))
    probs_b = jnp.exp(scores - log_total).astype(jnp.bfloat16)
    mixed = product('ihst,ithd->ishd', probs_b, valued).astype(jnp.bfloat16).reshape(total_rows, head_cols)
    partial_out = product('rc,oc->ro', mixed, weights[:, 3, :])
    return (partial_out, (queries, keyed, valued, log_total, mixed))

def attend_backward(upstream, normed_b, weights, saved):
    queries, keyed, valued, log_total, mixed = saved
    total_rows, head_cols = mixed.shape
    scaling = HD ** (-0.5)
    upstream_b = upstream.astype(jnp.bfloat16)
    grad_out_w = product('ro,rc->oc', upstream_b, mixed)
    grad_mixed = product('ro,oc->rc', upstream_b, weights[:, 3, :]).astype(jnp.bfloat16).reshape(queries.shape)
    scores = product('ishd,ithd->ihst', queries, keyed) * scaling
    probs = jnp.exp(scores - log_total)
    grad_value = product('ihst,ishd->ithd', probs.astype(jnp.bfloat16), grad_mixed).astype(jnp.bfloat16).reshape(total_rows, head_cols)
    grad_probs = product('ishd,ithd->ihst', grad_mixed, valued)
    inner = lax.optimization_barrier(jnp.sum(probs * grad_probs, axis=-1, keepdims=True))
    grad_score = (probs * (grad_probs - inner)).astype(jnp.bfloat16)
    grad_query = (product('ihst,ithd->ishd', grad_score, keyed) * scaling).astype(jnp.bfloat16).reshape(total_rows, head_cols)
    grad_key = (product('ihst,ishd->ithd', grad_score, queries) * scaling).astype(jnp.bfloat16).reshape(total_rows, head_cols)
    grad_weights = jnp.stack([product('rd,rc->dc', normed_b, grad_query), product('rd,rc->dc', normed_b, grad_key), product('rd,rc->dc', normed_b, grad_value), grad_out_w], axis=1)
    partial_in = product('rc,dc->rd', grad_query, weights[:, 0, :]) + product('rc,dc->rd', grad_key, weights[:, 1, :]) + product('rc,dc->rd', grad_value, weights[:, 2, :])
    return (partial_in, grad_weights)

def device_block(weights, tokens, cotangent, expert_ids, count):
    w_attn, norm_gain, norm_bias, mlp_in, mlp_out, router, exp_in, exp_out = weights
    total_rows, width = tokens.shape
    images = total_rows // SEQ
    experts = router.shape[1]
    live = (jnp.arange(total_rows, dtype=jnp.int32) // SEQ < count).astype(jnp.int32)
    live_f = live.astype(jnp.float32)
    gain_all = norm_gain.astype(jnp.float32)
    bias_all = norm_bias.astype(jnp.float32)
    normed, unit_a0, inverse_a0 = norm_forward(tokens, gain_all[0, 0], bias_all[0, 0])
    first_zero = normed.astype(jnp.bfloat16)
    attn_out, saved_zero = attend_forward(first_zero, w_attn[0], images)
    middle_zero = tokens + attn_out
    normed, unit_c0, inverse_c0 = norm_forward(middle_zero, gain_all[0, 1], bias_all[0, 1])
    second_zero = normed.astype(jnp.bfloat16)
    before_dense = product('rd,df->rf', second_zero, mlp_in)
    hidden_dense = gelu_value(before_dense).astype(jnp.bfloat16)
    after_zero = middle_zero + product('rf,df->rd', hidden_dense, mlp_out)
    normed, unit_a1, inverse_a1 = norm_forward(after_zero, gain_all[1, 0], bias_all[1, 0])
    first_one = normed.astype(jnp.bfloat16)
    attn_out, saved_one = attend_forward(first_one, w_attn[1], images)
    middle_one = after_zero + attn_out
    normed, unit_c1, inverse_c1 = norm_forward(middle_one, gain_all[1, 1], bias_all[1, 1])
    second_one = normed.astype(jnp.bfloat16)
    probs = jax.nn.softmax(product('rd,de->re', second_one, router), axis=-1)
    gate = jnp.take_along_axis(probs, expert_ids, axis=1) * live_f[:, None]
    target = route_slots(expert_ids, live, experts, CAP)
    routed = jnp.zeros((experts * CAP, width), jnp.bfloat16).at[target.reshape(-1)].set(jnp.repeat(second_one, expert_ids.shape[1], axis=0), mode='drop').reshape(experts, CAP, width)
    before_exp = product('ecd,edf->ecf', routed, exp_in)
    hidden_exp = gelu_value(before_exp).astype(jnp.bfloat16)
    expert_out = product('ecf,edf->ecd', hidden_exp, exp_out).reshape(experts * CAP, width)
    picked = jnp.take(expert_out, target, axis=0, mode='fill', fill_value=0.0)
    output = middle_one + lax.optimization_barrier(jnp.sum(gate[:, :, None] * picked, axis=1))
    upstream = cotangent * live_f[:, None]
    grad_gate = lax.optimization_barrier(jnp.sum(upstream[:, None, :] * picked, axis=-1))
    sent = (gate[:, :, None] * upstream[:, None, :]).astype(jnp.bfloat16).reshape(-1, width)
    grad_routed = jnp.zeros((experts * CAP, width), jnp.bfloat16).at[target.reshape(-1)].set(sent, mode='drop').reshape(experts, CAP, width)
    grad_exp_out = product('ecd,ecf->edf', grad_routed, hidden_exp)
    grad_before = (product('ecd,edf->ecf', grad_routed, exp_out) * gelu_slope(before_exp)).astype(jnp.bfloat16)
    grad_exp_in = product('ecd,ecf->edf', routed, grad_before)
    routed_in = product('ecf,edf->ecd', grad_before, exp_in).reshape(experts * CAP, width)
    grad_second = lax.optimization_barrier(jnp.sum(jnp.take(routed_in, target, axis=0, mode='fill', fill_value=0.0), axis=1))
    onehot = (expert_ids[:, :, None] == jnp.arange(experts, dtype=jnp.int32)[None, None, :]).astype(jnp.float32)
    grad_probs = lax.optimization_barrier(jnp.sum(onehot * (grad_gate * live_f[:, None])[:, :, None], axis=1))
    grad_logits = (probs * (grad_probs - lax.optimization_barrier(jnp.sum(probs * grad_probs, axis=1, keepdims=True)))).astype(jnp.bfloat16)
    grad_router = product('rd,re->de', second_one, grad_logits)
    grad_second = grad_second + product('re,de->rd', grad_logits, router)
    norm_delta, gain_c1, bias_c1 = norm_backward(grad_second, unit_c1, inverse_c1, gain_all[1, 1])
    grad_middle = upstream + norm_delta
    grad_first, grad_attn_one = attend_backward(grad_middle, first_one, w_attn[1], saved_one)
    norm_delta, gain_a1, bias_a1 = norm_backward(grad_first, unit_a1, inverse_a1, gain_all[1, 0])
    grad_after = grad_middle + norm_delta
    upstream_b = grad_after.astype(jnp.bfloat16)
    grad_mlp_out = product('rd,rf->df', upstream_b, hidden_dense)
    grad_before_dense = (product('rd,df->rf', upstream_b, mlp_out) * gelu_slope(before_dense)).astype(jnp.bfloat16)
    grad_mlp_in = product('rd,rf->df', second_zero, grad_before_dense)
    grad_second_zero = product('rf,df->rd', grad_before_dense, mlp_in)
    norm_delta, gain_c0, bias_c0 = norm_backward(grad_second_zero, unit_c0, inverse_c0, gain_all[0, 1])
    grad_middle_zero = grad_after + norm_delta
    grad_first_zero, grad_attn_zero = attend_backward(grad_middle_zero, first_zero, w_attn[0], saved_zero)
    norm_delta, gain_a0, bias_a0 = norm_backward(grad_first_zero, unit_a0, inverse_a0, gain_all[0, 0])
    grad_input = grad_middle_zero + norm_delta
    grads = (jnp.stack([grad_attn_zero, grad_attn_one]), jnp.stack([jnp.stack([gain_a0, gain_c0]), jnp.stack([gain_a1, gain_c1])]), jnp.stack([jnp.stack([bias_a0, bias_c0]), jnp.stack([bias_a1, bias_c1])]), grad_mlp_in, grad_mlp_out, grad_router, grad_exp_in, grad_exp_out)
    return (output, grad_input, grads)

def reference(tokens, cotangent, expert_ids, image_counts, w_attn, norm_gain, norm_bias, mlp_in, mlp_out, router, exp_in, exp_out):
    weights = (w_attn, norm_gain, norm_bias, mlp_in, mlp_out, router, exp_in, exp_out)
    block_rows = IMG_DEV * SEQ
    width = tokens.shape[1]
    blocks = tokens.shape[0] // block_rows
    stacked = (tokens.reshape(blocks, block_rows, width), cotangent.reshape(blocks, block_rows, width), expert_ids.reshape(blocks, block_rows, expert_ids.shape[1]), image_counts)
    initial = tuple((jnp.zeros(weight.shape, jnp.float32) for weight in weights))

    def advance(carry, inputs):
        output, grad_input, grads = device_block(weights, inputs[0], inputs[1], inputs[2], inputs[3])
        return (tuple((total + grad for total, grad in zip(carry, grads))), (output, grad_input))
    totals, (outputs, grad_inputs) = lax.scan(advance, initial, stacked)
    return (outputs.reshape(-1, width), grad_inputs.reshape(-1, width), totals[0], totals[1], totals[2], totals[3], totals[4], totals[5], totals[6], totals[7])
```

```python
import jax
import jax.numpy as jnp
from jax import lax
from jax.experimental import pallas as pl
from jax.experimental.pallas import tpu as pltpu
from jax.sharding import PartitionSpec as P

HD = 64
SEQ = 197


EPS = 1e-06
ROOT_HALF = 0.7071067811865476
INV_ROOT_TAU = 0.3989422804014327


def product(form, left, right):
    return jnp.einsum(form, left, right, preferred_element_type=jnp.float32)


def gelu_value(values):
    return values * 0.5 * (1.0 + lax.erf(values * ROOT_HALF))


def gelu_slope(values):
    return (
        0.5 * (1.0 + lax.erf(values * ROOT_HALF))
        + values * jnp.exp(-0.5 * values * values) * INV_ROOT_TAU
    )


def norm_forward(inputs, weight_gain, weight_bias):
    center = inputs - jnp.mean(inputs, axis=-1, keepdims=True)
    inverse = lax.rsqrt(jnp.mean(center * center, axis=-1, keepdims=True) + EPS)
    normed = center * inverse
    return (normed * weight_gain + weight_bias, normed, inverse)


def norm_backward(upstream, normed, inverse, weight_gain):
    scaled = upstream * weight_gain
    result = inverse * (
        scaled
        - jnp.mean(scaled, axis=-1, keepdims=True)
        - normed * jnp.mean(scaled * normed, axis=-1, keepdims=True)
    )
    return (result, jnp.sum(upstream * normed, axis=0), jnp.sum(upstream, axis=0))


def sum_kernel(x_ref, o_ref, landed, send_a, recv_a, send_b, recv_b):
    members = x_ref.shape[0]
    me = lax.axis_index("tensor")
    peers = [lax.rem(me + d, members) for d in range(1, members)]
    barrier = pltpu.get_barrier_semaphore()
    for peer in peers:
        pl.semaphore_signal(
            barrier, inc=1, device_id={"tensor": peer}, device_id_type=pl.DeviceIdType.MESH
        )
    pl.semaphore_wait(barrier, members - 1)
    first = [
        pltpu.make_async_remote_copy(
            src_ref=x_ref.at[peer],
            dst_ref=landed.at[d],
            send_sem=send_a.at[d],
            recv_sem=recv_a.at[d],
            device_id={"tensor": peer},
            device_id_type=pl.DeviceIdType.MESH,
        )
        for d, peer in enumerate(peers)
    ]
    for copy in first:
        copy.start()
    total = x_ref[me].astype(jnp.float32)
    for d, copy in enumerate(first):
        copy.wait_recv()
        total = total + landed[d].astype(jnp.float32)
    o_ref[me] = total.astype(jnp.bfloat16)
    second = [
        pltpu.make_async_remote_copy(
            src_ref=o_ref.at[me],
            dst_ref=o_ref.at[me],
            send_sem=send_b.at[d],
            recv_sem=recv_b.at[d],
            device_id={"tensor": peer},
            device_id_type=pl.DeviceIdType.MESH,
        )
        for d, peer in enumerate(peers)
    ]
    for copy in second:
        copy.start()
    for copy in first:
        copy.wait_send()
    for copy in second:
        copy.wait()


def tensor_sum(partial, ident):
    members = lax.axis_size("tensor")
    rows, cols = partial.shape
    chunk = 8 * ((rows + 8 * members - 1) // (8 * members))
    padded = jnp.pad(partial.astype(jnp.bfloat16), ((0, members * chunk - rows), (0, 0)))
    shape = (members, chunk, cols)
    dma = pltpu.SemaphoreType.DMA((members - 1,))
    summed = pl.pallas_call(
        sum_kernel,
        out_shape=jax.ShapeDtypeStruct(shape, jnp.bfloat16),
        in_specs=[pl.BlockSpec(memory_space=pltpu.VMEM)],
        out_specs=pl.BlockSpec(memory_space=pltpu.VMEM),
        scratch_shapes=[pltpu.VMEM((members - 1, chunk, cols), jnp.bfloat16), dma, dma, dma, dma],
        compiler_params=pltpu.CompilerParams(collective_id=ident, has_side_effects=True),
        cost_estimate=pl.CostEstimate(
            flops=0, bytes_accessed=80 * rows * cols * 2, transcendentals=0
        ),
    )(padded.reshape(shape))
    return summed.reshape(members * chunk, cols)[:rows].astype(jnp.float32)


def route_slots(expert_ids, live, experts, capacity):
    flat_ids = expert_ids.reshape(-1)
    flat_live = jnp.repeat(live, expert_ids.shape[1])
    onehot = (flat_ids[:, None] == jnp.arange(experts, dtype=jnp.int32)[None, :]).astype(
        jnp.int32
    ) * flat_live[:, None]
    earlier = jnp.cumsum(onehot, axis=0) - onehot
    position = jnp.sum(earlier * onehot, axis=1)
    target = jnp.where(flat_live > 0, flat_ids * capacity + position, experts * capacity)
    return target.reshape(expert_ids.shape)


def slot_count(block_rows, experts, hidden_local):
    groups = lax.axis_size("fsdp")
    by_rows = 8 * (block_rows * 10 // (experts * 32) + 1)
    by_width = 8 * ((hidden_local + 8 * groups - 1) // (8 * groups))
    return max(by_rows, by_width)


def attend_forward(normed_b, weights, images):
    total_rows = normed_b.shape[0]
    head_cols = weights.shape[1] // 4
    scaling = HD ** (-0.5)
    shaped = (images, total_rows // images, head_cols // HD, HD)
    joined = product("rd,dc->rc", normed_b, weights[:, : 3 * head_cols]).astype(jnp.bfloat16)
    queries, keyed, valued = (
        joined[:, j * head_cols : (j + 1) * head_cols].reshape(shaped) for j in range(3)
    )
    scores = product("ishd,ithd->ihst", queries, keyed) * scaling
    highest = jnp.max(scores, axis=-1, keepdims=True)
    log_total = highest + jnp.log(jnp.sum(jnp.exp(scores - highest), axis=-1, keepdims=True))
    probs_b = jnp.exp(scores - log_total).astype(jnp.bfloat16)
    mixed = (
        product("ihst,ithd->ishd", probs_b, valued)
        .astype(jnp.bfloat16)
        .reshape(total_rows, head_cols)
    )
    partial_out = product("rc,oc->ro", mixed, weights[:, 3 * head_cols :])
    return (tensor_sum(partial_out, 0), (queries, keyed, valued, log_total, mixed))


def attend_backward(upstream, normed_b, weights, saved):
    queries, keyed, valued, log_total, mixed = saved
    total_rows, head_cols = mixed.shape
    scaling = HD ** (-0.5)
    upstream_b = upstream.astype(jnp.bfloat16)
    grad_out_w = product("ro,rc->oc", upstream_b, mixed)
    grad_mixed = (
        product("ro,oc->rc", upstream_b, weights[:, 3 * head_cols :])
        .astype(jnp.bfloat16)
        .reshape(queries.shape)
    )
    scores = product("ishd,ithd->ihst", queries, keyed) * scaling
    probs = jnp.exp(scores - log_total)
    grad_value = (
        product("ihst,ishd->ithd", probs.astype(jnp.bfloat16), grad_mixed)
        .astype(jnp.bfloat16)
        .reshape(total_rows, head_cols)
    )
    grad_probs = product("ishd,ithd->ihst", grad_mixed, valued)
    inner = jnp.sum(probs * grad_probs, axis=-1, keepdims=True)
    grad_score = (probs * (grad_probs - inner)).astype(jnp.bfloat16)
    grad_query = (
        (product("ihst,ithd->ishd", grad_score, keyed) * scaling)
        .astype(jnp.bfloat16)
        .reshape(total_rows, head_cols)
    )
    grad_key = (
        (product("ihst,ishd->ithd", grad_score, queries) * scaling)
        .astype(jnp.bfloat16)
        .reshape(total_rows, head_cols)
    )
    grad_joined = jnp.concatenate([grad_query, grad_key, grad_value], axis=1)
    grad_weights = jnp.concatenate(
        [product("rd,rc->dc", normed_b, grad_joined), grad_out_w], axis=1
    ).astype(jnp.bfloat16)
    partial_in = product("rc,dc->rd", grad_joined, weights[:, : 3 * head_cols])
    return (tensor_sum(partial_in, 0), grad_weights)


def dense_forward(normed_b, up_weight, down_weight):
    before = product("rd,df->rf", normed_b, up_weight)
    hidden_b = gelu_value(before).astype(jnp.bfloat16)
    partial_out = product("rf,df->rd", hidden_b, down_weight)
    return (tensor_sum(partial_out, 0), (before, hidden_b))


def dense_backward(upstream, normed_b, up_weight, down_weight, saved):
    before, hidden_b = saved
    upstream_b = upstream.astype(jnp.bfloat16)
    grad_down = product("rd,rf->df", upstream_b, hidden_b)
    grad_before = (product("rd,df->rf", upstream_b, down_weight) * gelu_slope(before)).astype(
        jnp.bfloat16
    )
    grad_up = product("rd,rf->df", normed_b, grad_before)
    partial_in = product("rf,df->rd", grad_before, up_weight)
    return (
        tensor_sum(partial_in, 0),
        grad_up,
        grad_down,
    )


def expert_forward(normed_b, router_w, in_weight, out_weight, expert_ids, live):
    total_rows, width = normed_b.shape
    experts = router_w.shape[1]
    capacity = slot_count(total_rows, experts, in_weight.shape[2])
    live_f = live.astype(jnp.float32)
    onehot = (expert_ids[:, :, None] == jnp.arange(experts, dtype=jnp.int32)[None, None, :]).astype(
        jnp.float32
    )
    probs = jax.nn.softmax(product("rd,de->re", normed_b, router_w), axis=-1)
    gate = jnp.sum(probs[:, None, :] * onehot, axis=-1) * live_f[:, None]
    target = route_slots(expert_ids, live, experts, capacity)
    slots = jnp.arange(experts * capacity, dtype=jnp.int32)[:, None]
    hits = [slots == target[:, k][None, :] for k in range(target.shape[1])]
    place = sum(hit.astype(jnp.bfloat16) for hit in hits)
    slot_gate = sum(jnp.sum(jnp.where(hit, gate[:, k][None, :], 0.0), axis=1) for k, hit in enumerate(hits))
    routed = product("sr,rd->sd", place, normed_b).astype(jnp.bfloat16)
    routed = routed.reshape(experts, capacity, width)
    before = product("ecd,edf->ecf", routed, in_weight)
    hidden_b = gelu_value(before).astype(jnp.bfloat16)
    expert_part = product("ecf,edf->ecd", hidden_b, out_weight).reshape(experts * capacity, width)
    weighted = (slot_gate[:, None] * expert_part).astype(jnp.bfloat16)
    mixed = product("sr,sd->rd", place, weighted).astype(jnp.bfloat16)
    return (mixed, (onehot, probs, place, target, slot_gate, routed, before, hidden_b, expert_part))


def expert_backward(upstream, normed_b, router_w, in_weight, out_weight, live, saved):
    onehot, probs, place, target, slot_gate, routed, before, hidden_b, expert_part = saved
    experts, capacity, width = routed.shape
    total_rows = normed_b.shape[0]
    live_f = live.astype(jnp.float32)
    carried = product("sr,rd->sd", place, upstream.astype(jnp.bfloat16))
    slot_part = jnp.sum(carried * expert_part, axis=1)
    slots = jnp.arange(experts * capacity, dtype=jnp.int32)[None, :]
    gate_part = jnp.stack(
        [
            jnp.sum(jnp.where(slots == target[:, k][:, None], slot_part[None, :], 0.0), axis=1)
            for k in range(target.shape[1])
        ],
        axis=1,
    )
    grad_routed = (
        (slot_gate[:, None] * carried).astype(jnp.bfloat16).reshape(experts, capacity, width)
    )
    grad_out_w = product("ecd,ecf->edf", grad_routed, hidden_b).astype(jnp.bfloat16)
    grad_before = (product("ecd,edf->ecf", grad_routed, out_weight) * gelu_slope(before)).astype(
        jnp.bfloat16
    )
    grad_in_w = product("ecd,ecf->edf", routed, grad_before).astype(jnp.bfloat16)
    partial_in = product("ecf,edf->ecd", grad_before, in_weight).reshape(experts * capacity, width)
    token_part = product("sr,sd->rd", place, partial_in.astype(jnp.bfloat16))
    both = jnp.concatenate(
        [token_part, jnp.pad(gate_part, ((0, 0), (0, 128 - gate_part.shape[1])))], axis=1
    ).astype(jnp.bfloat16)
    both, grad_out_w, grad_in_w = lax.optimization_barrier((both, grad_out_w, grad_in_w))
    summed = tensor_sum(both, 1)
    grad_tokens = summed[:, :width]
    grad_gate = summed[:, width : width + gate_part.shape[1]]
    grad_probs = jnp.sum(onehot * (grad_gate * live_f[:, None])[:, :, None], axis=1)
    grad_logits = (
        probs * (grad_probs - jnp.sum(probs * grad_probs, axis=1, keepdims=True))
    ).astype(jnp.bfloat16)
    grad_router = product("rd,re->de", normed_b, grad_logits)
    grad_tokens = grad_tokens + product("re,de->rd", grad_logits, router_w)
    return (grad_tokens, grad_router, grad_in_w, grad_out_w)


def per_device(
    tokens,
    cotangent,
    expert_ids,
    image_counts,
    w_attn,
    norm_gain,
    norm_bias,
    mlp_in,
    mlp_out,
    router,
    exp_in,
    exp_out,
):
    total_rows = tokens.shape[0]
    images = total_rows // SEQ
    live = (jnp.arange(total_rows, dtype=jnp.int32) // SEQ < image_counts[0]).astype(jnp.int32)
    width_local = norm_gain.shape[2]
    heads = w_attn.shape[2] * w_attn.shape[3]
    hidden = mlp_in.shape[1]
    experts = router.shape[1]
    small = jnp.concatenate(
        [norm_gain.reshape(-1, width_local).T, norm_bias.reshape(-1, width_local).T, router], axis=1
    )
    extra = -small.shape[1] % 128
    small = jnp.pad(small, ((0, 0), (0, extra)))
    packed = jnp.concatenate(
        [
            w_attn[0].reshape(width_local, heads),
            w_attn[1].reshape(width_local, heads),
            mlp_in,
            mlp_out,
            small,
        ],
        axis=1,
    )
    whole = lax.all_gather(packed, "fsdp", axis=0, tiled=True)
    whole, exp_in, exp_out = lax.optimization_barrier((whole, exp_in, exp_out))
    in_full = lax.all_gather(exp_in, "fsdp", axis=1, tiled=True)
    out_full = lax.all_gather(exp_out, "fsdp", axis=1, tiled=True)
    attn_w = (whole[:, :heads], whole[:, heads : 2 * heads])
    up_w = whole[:, 2 * heads : 2 * heads + hidden]
    down_w = whole[:, 2 * heads + hidden : 2 * heads + 2 * hidden]
    rest = whole[:, 2 * heads + 2 * hidden :]
    gains = rest[:, :4].astype(jnp.float32).T.reshape(2, 2, -1)
    biases = rest[:, 4:8].astype(jnp.float32).T.reshape(2, 2, -1)
    router_w = rest[:, 8 : 8 + experts]

    normed, unit_a0, inverse_a0 = norm_forward(tokens, gains[0, 0], biases[0, 0])
    first_zero = normed.astype(jnp.bfloat16)
    attn_out, saved_attn_zero = attend_forward(first_zero, attn_w[0], images)
    middle_zero = tokens + attn_out
    normed, unit_c0, inverse_c0 = norm_forward(middle_zero, gains[0, 1], biases[0, 1])
    second_zero = normed.astype(jnp.bfloat16)
    dense_out, saved_dense = dense_forward(second_zero, up_w, down_w)
    after_zero = middle_zero + dense_out
    normed, unit_a1, inverse_a1 = norm_forward(after_zero, gains[1, 0], biases[1, 0])
    first_one = normed.astype(jnp.bfloat16)
    attn_out, saved_attn_one = attend_forward(first_one, attn_w[1], images)
    middle_one = after_zero + attn_out
    normed, unit_c1, inverse_c1 = norm_forward(middle_one, gains[1, 1], biases[1, 1])
    second_one = normed.astype(jnp.bfloat16)
    mixed, saved_moe = expert_forward(
        second_one, router_w, in_full, out_full, expert_ids, live
    )
    output = middle_one + lax.psum(mixed, "tensor").astype(jnp.float32)
    upstream = cotangent * live.astype(jnp.float32)[:, None]
    grad_second, grad_router, grad_exp_in, grad_exp_out = expert_backward(
        upstream, second_one, router_w, in_full, out_full, live, saved_moe
    )
    grad_exp_out = lax.psum_scatter(grad_exp_out, "fsdp", scatter_dimension=1, tiled=True)
    grad_exp_in = lax.psum_scatter(grad_exp_in, "fsdp", scatter_dimension=1, tiled=True)
    norm_delta, gain_c1, bias_c1 = norm_backward(grad_second, unit_c1, inverse_c1, gains[1, 1])
    grad_middle = upstream + norm_delta
    grad_first, grad_attn_one = attend_backward(grad_middle, first_one, attn_w[1], saved_attn_one)
    norm_delta, gain_a1, bias_a1 = norm_backward(grad_first, unit_a1, inverse_a1, gains[1, 0])
    grad_after = grad_middle + norm_delta
    grad_second_zero, grad_mlp_in, grad_mlp_out = dense_backward(
        grad_after, second_zero, up_w, down_w, saved_dense
    )
    norm_delta, gain_c0, bias_c0 = norm_backward(
        grad_second_zero, unit_c0, inverse_c0, gains[0, 1]
    )
    grad_middle_zero = grad_after + norm_delta
    grad_first_zero, grad_attn_zero = attend_backward(
        grad_middle_zero, first_zero, attn_w[0], saved_attn_zero
    )
    norm_delta, gain_a0, bias_a0 = norm_backward(
        grad_first_zero, unit_a0, inverse_a0, gains[0, 0]
    )
    grad_input = grad_middle_zero + norm_delta
    vectors = [gain_a0, gain_c0, gain_a1, gain_c1, bias_a0, bias_c0, bias_a1, bias_c1]
    small_grad = jnp.concatenate([jnp.stack(vectors, axis=1), grad_router], axis=1)
    small_grad = jnp.pad(small_grad, ((0, 0), (0, extra))).astype(jnp.bfloat16)
    packed_grad = jnp.concatenate(
        [
            grad_attn_zero,
            grad_attn_one,
            grad_mlp_in.astype(jnp.bfloat16),
            grad_mlp_out.astype(jnp.bfloat16),
            small_grad,
        ],
        axis=1,
    )
    packed_grad, grad_exp_in, grad_exp_out = lax.optimization_barrier(
        (packed_grad, grad_exp_in, grad_exp_out)
    )
    owned = lax.psum_scatter(packed_grad, "fsdp", scatter_dimension=0, tiled=True).astype(
        jnp.float32
    )
    grad_attn = jnp.stack(
        [
            owned[:, :heads].reshape(w_attn.shape[1:]),
            owned[:, heads : 2 * heads].reshape(w_attn.shape[1:]),
        ]
    )
    tail = owned[:, 2 * heads + 2 * hidden :]
    return (
        output,
        grad_input,
        grad_attn,
        tail[:, :4].T.reshape(norm_gain.shape),
        tail[:, 4:8].T.reshape(norm_bias.shape),
        owned[:, 2 * heads : 2 * heads + hidden],
        owned[:, 2 * heads + hidden : 2 * heads + 2 * hidden],
        tail[:, 8 : 8 + experts],
        grad_exp_in.astype(jnp.float32),
        grad_exp_out.astype(jnp.float32),
    )


def solution(mesh):
    in_specs = (
        P("fsdp", None),
        P("fsdp", None),
        P("fsdp", None),
        P("fsdp"),
        P(None, "fsdp", None, "tensor"),
        P(None, None, "fsdp"),
        P(None, None, "fsdp"),
        P("fsdp", "tensor"),
        P("fsdp", "tensor"),
        P("fsdp", None),
        P(None, "fsdp", "tensor"),
        P(None, "fsdp", "tensor"),
    )
    out_specs = (
        P("fsdp", None),
        P("fsdp", None),
        P(None, "fsdp", None, "tensor"),
        P(None, None, "fsdp"),
        P(None, None, "fsdp"),
        P("fsdp", "tensor"),
        P("fsdp", "tensor"),
        P("fsdp", None),
        P(None, "fsdp", "tensor"),
        P(None, "fsdp", "tensor"),
    )
    return jax.shard_map(
        per_device, mesh=mesh, in_specs=in_specs, out_specs=out_specs, check_vma=False
    )
```

```python
import jax
import jax.numpy as jnp
from jax import lax
from jax.experimental import pallas as pl
from jax.experimental.layout import Layout, with_layout_constraint
from jax.experimental.pallas import tpu as pltpu
from jax.sharding import PartitionSpec as P

HD = 64
SEQ = 197


EPS = 1e-06
ROOT_HALF = 0.7071067811865476
INV_ROOT_TAU = 0.3989422804014327


def product(form, left, right):
    return jnp.einsum(form, left, right, preferred_element_type=jnp.float32)


def gelu_value(values):
    return values * 0.5 * (1.0 + lax.erf(values * ROOT_HALF))


def gelu_slope(values):
    return (
        0.5 * (1.0 + lax.erf(values * ROOT_HALF))
        + values * jnp.exp(-0.5 * values * values) * INV_ROOT_TAU
    )


def norm_forward(inputs, weight_gain, weight_bias):
    center = inputs - jnp.mean(inputs, axis=-1, keepdims=True)
    inverse = lax.rsqrt(jnp.mean(center * center, axis=-1, keepdims=True) + EPS)
    normed = center * inverse
    return (normed * weight_gain + weight_bias, normed, inverse)


def norm_backward(upstream, normed, inverse, weight_gain):
    scaled = upstream * weight_gain
    result = inverse * (
        scaled
        - jnp.mean(scaled, axis=-1, keepdims=True)
        - normed * jnp.mean(scaled * normed, axis=-1, keepdims=True)
    )
    return (result, jnp.sum(upstream * normed, axis=0), jnp.sum(upstream, axis=0))


def sum_kernel(x_ref, o_ref, landed, send_a, recv_a, send_b, recv_b):
    members = x_ref.shape[0]
    me = lax.axis_index("tensor")
    peers = [lax.rem(me + d, members) for d in range(1, members)]
    barrier = pltpu.get_barrier_semaphore()
    for peer in peers:
        pl.semaphore_signal(
            barrier, inc=1, device_id={"tensor": peer}, device_id_type=pl.DeviceIdType.MESH
        )
    pl.semaphore_wait(barrier, members - 1)
    first = [
        pltpu.make_async_remote_copy(
            src_ref=x_ref.at[peer],
            dst_ref=landed.at[d],
            send_sem=send_a.at[d],
            recv_sem=recv_a.at[d],
            device_id={"tensor": peer},
            device_id_type=pl.DeviceIdType.MESH,
        )
        for d, peer in enumerate(peers)
    ]
    for copy in first:
        copy.start()
    total = x_ref[me].astype(jnp.float32)
    for d, copy in enumerate(first):
        copy.wait_recv()
        total = total + landed[d].astype(jnp.float32)
    o_ref[me] = total.astype(jnp.bfloat16)
    second = [
        pltpu.make_async_remote_copy(
            src_ref=o_ref.at[me],
            dst_ref=o_ref.at[me],
            send_sem=send_b.at[d],
            recv_sem=recv_b.at[d],
            device_id={"tensor": peer},
            device_id_type=pl.DeviceIdType.MESH,
        )
        for d, peer in enumerate(peers)
    ]
    for copy in second:
        copy.start()
    for copy in first:
        copy.wait_send()
    for copy in second:
        copy.wait()


def tensor_sum(partial, ident):
    members = lax.axis_size("tensor")
    rows, cols = partial.shape
    chunk = 8 * ((rows + 8 * members - 1) // (8 * members))
    padded = jnp.pad(partial.astype(jnp.bfloat16), ((0, members * chunk - rows), (0, 0)))
    shape = (members, chunk, cols)
    dma = pltpu.SemaphoreType.DMA((members - 1,))
    summed = pl.pallas_call(
        sum_kernel,
        out_shape=jax.ShapeDtypeStruct(shape, jnp.bfloat16),
        in_specs=[pl.BlockSpec(memory_space=pltpu.VMEM)],
        out_specs=pl.BlockSpec(memory_space=pltpu.VMEM),
        scratch_shapes=[pltpu.VMEM((members - 1, chunk, cols), jnp.bfloat16), dma, dma, dma, dma],
        compiler_params=pltpu.CompilerParams(collective_id=ident, has_side_effects=True),
        cost_estimate=pl.CostEstimate(
            flops=0, bytes_accessed=80 * rows * cols * 2, transcendentals=0
        ),
    )(padded.reshape(shape))
    return summed.reshape(members * chunk, cols)[:rows].astype(jnp.float32)


def route_slots(expert_ids, live, experts, capacity):
    flat_ids = expert_ids.reshape(-1)
    flat_live = jnp.repeat(live, expert_ids.shape[1])
    onehot = (flat_ids[:, None] == jnp.arange(experts, dtype=jnp.int32)[None, :]).astype(
        jnp.int32
    ) * flat_live[:, None]
    earlier = jnp.cumsum(onehot, axis=0) - onehot
    position = jnp.sum(earlier * onehot, axis=1)
    target = jnp.where(flat_live > 0, flat_ids * capacity + position, experts * capacity)
    return target.reshape(expert_ids.shape)


def slot_count(block_rows, experts, hidden_local):
    groups = lax.axis_size("fsdp")
    by_rows = 8 * (block_rows * 10 // (experts * 32) + 1)
    by_width = 8 * ((hidden_local + 8 * groups - 1) // (8 * groups))
    return max(by_rows, by_width)


def attend_forward(normed_b, weights, images):
    total_rows = normed_b.shape[0]
    head_cols = weights.shape[1] // 4
    scaling = HD ** (-0.5)
    shaped = (images, total_rows // images, head_cols // HD, HD)
    joined = product("rd,dc->rc", normed_b, weights[:, : 3 * head_cols]).astype(jnp.bfloat16)
    queries, keyed, valued = (
        joined[:, j * head_cols : (j + 1) * head_cols].reshape(shaped) for j in range(3)
    )
    scores = product("ishd,ithd->ihst", queries, keyed) * scaling
    highest = jnp.max(scores, axis=-1, keepdims=True)
    log_total = highest + jnp.log(jnp.sum(jnp.exp(scores - highest), axis=-1, keepdims=True))
    probs_b = jnp.exp(scores - log_total).astype(jnp.bfloat16)
    mixed = (
        product("ihst,ithd->ishd", probs_b, valued)
        .astype(jnp.bfloat16)
        .reshape(total_rows, head_cols)
    )
    partial_out = product("rc,oc->ro", mixed, weights[:, 3 * head_cols :])
    return (tensor_sum(partial_out, 0), (queries, keyed, valued, log_total, mixed))


def attend_backward(upstream, normed_b, weights, saved):
    queries, keyed, valued, log_total, mixed = saved
    total_rows, head_cols = mixed.shape
    scaling = HD ** (-0.5)
    upstream_b = upstream.astype(jnp.bfloat16)
    grad_out_w = product("ro,rc->oc", upstream_b, mixed)
    grad_mixed = (
        product("ro,oc->rc", upstream_b, weights[:, 3 * head_cols :])
        .astype(jnp.bfloat16)
        .reshape(queries.shape)
    )
    scores = product("ishd,ithd->ihst", queries, keyed) * scaling
    probs = jnp.exp(scores - log_total)
    grad_value = (
        product("ihst,ishd->ithd", probs.astype(jnp.bfloat16), grad_mixed)
        .astype(jnp.bfloat16)
        .reshape(total_rows, head_cols)
    )
    grad_probs = product("ishd,ithd->ihst", grad_mixed, valued)
    inner = jnp.sum(probs * grad_probs, axis=-1, keepdims=True)
    grad_score = (probs * (grad_probs - inner)).astype(jnp.bfloat16)
    grad_query = (
        (product("ihst,ithd->ishd", grad_score, keyed) * scaling)
        .astype(jnp.bfloat16)
        .reshape(total_rows, head_cols)
    )
    grad_key = (
        (product("ihst,ishd->ithd", grad_score, queries) * scaling)
        .astype(jnp.bfloat16)
        .reshape(total_rows, head_cols)
    )
    grad_joined = jnp.concatenate([grad_query, grad_key, grad_value], axis=1)
    grad_weights = jnp.concatenate(
        [product("rd,rc->dc", normed_b, grad_joined), grad_out_w], axis=1
    ).astype(jnp.bfloat16)
    partial_in = product("rc,dc->rd", grad_joined, weights[:, : 3 * head_cols])
    return (tensor_sum(partial_in, 0), grad_weights)


def dense_forward(normed_b, up_weight, down_weight):
    before = product("rd,df->rf", normed_b, up_weight)
    hidden_b = gelu_value(before).astype(jnp.bfloat16)
    partial_out = product("rf,df->rd", hidden_b, down_weight)
    return (tensor_sum(partial_out, 0), (before, hidden_b))


def dense_backward(upstream, normed_b, up_weight, down_weight, saved):
    before, hidden_b = saved
    upstream_b = upstream.astype(jnp.bfloat16)
    grad_down = product("rd,rf->df", upstream_b, hidden_b)
    grad_before = (product("rd,df->rf", upstream_b, down_weight) * gelu_slope(before)).astype(
        jnp.bfloat16
    )
    grad_up = product("rd,rf->df", normed_b, grad_before)
    partial_in = product("rf,df->rd", grad_before, up_weight)
    return (
        tensor_sum(partial_in, 0),
        grad_up,
        grad_down,
    )


def expert_forward(normed_b, router_w, in_weight, out_weight, expert_ids, live, upstream):
    total_rows, width = normed_b.shape
    experts = router_w.shape[1]
    capacity = slot_count(total_rows, experts, in_weight.shape[2])
    live_f = live.astype(jnp.float32)
    onehot = (expert_ids[:, :, None] == jnp.arange(experts, dtype=jnp.int32)[None, None, :]).astype(
        jnp.float32
    )
    probs = jax.nn.softmax(product("rd,de->re", normed_b, router_w), axis=-1)
    gate = jnp.sum(probs[:, None, :] * onehot, axis=-1) * live_f[:, None]
    target = route_slots(expert_ids, live, experts, capacity)
    slots = jnp.arange(experts * capacity, dtype=jnp.int32)[:, None]
    hits = [slots == target[:, k][None, :] for k in range(target.shape[1])]
    place = sum(hit.astype(jnp.bfloat16) for hit in hits)
    slot_gate = sum(jnp.sum(jnp.where(hit, gate[:, k][None, :], 0.0), axis=1) for k, hit in enumerate(hits))
    routed = product("sr,rd->sd", place, normed_b).astype(jnp.bfloat16)
    routed = routed.reshape(experts, capacity, width)
    before = product("ecd,edf->ecf", routed, in_weight)
    hidden_b = gelu_value(before).astype(jnp.bfloat16)
    carried = product("sr,rd->sd", place, upstream.astype(jnp.bfloat16))
    grad_routed = (
        (slot_gate[:, None] * carried).astype(jnp.bfloat16).reshape(experts, capacity, width)
    )
    grad_out_w = product("ecd,ecf->edf", grad_routed, hidden_b).astype(jnp.bfloat16)
    grad_out_w, out_weight = lax.optimization_barrier((grad_out_w, out_weight))
    grad_out_w = lax.psum_scatter(grad_out_w, "fsdp", scatter_dimension=1, tiled=True)
    expert_part = product("ecf,edf->ecd", hidden_b, out_weight).reshape(experts * capacity, width)
    weighted = (slot_gate[:, None] * expert_part).astype(jnp.bfloat16)
    mixed = product("sr,sd->rd", place, weighted).astype(jnp.bfloat16)
    saved = (onehot, probs, place, target, carried, grad_routed, routed, before, expert_part)
    return (mixed, grad_out_w, out_weight, saved)


def expert_backward(normed_b, router_w, in_weight, out_weight, live, saved):
    onehot, probs, place, target, carried, grad_routed, routed, before, expert_part = saved
    experts, capacity, width = routed.shape
    live_f = live.astype(jnp.float32)
    slot_part = jnp.sum(carried * expert_part, axis=1)
    slots = jnp.arange(experts * capacity, dtype=jnp.int32)[None, :]
    gate_part = jnp.stack(
        [
            jnp.sum(jnp.where(slots == target[:, k][:, None], slot_part[None, :], 0.0), axis=1)
            for k in range(target.shape[1])
        ],
        axis=1,
    )
    grad_before = (product("ecd,edf->ecf", grad_routed, out_weight) * gelu_slope(before)).astype(
        jnp.bfloat16
    )
    grad_in_w = product("ecd,ecf->edf", routed, grad_before).astype(jnp.bfloat16)
    partial_in = product("ecf,edf->ecd", grad_before, in_weight).reshape(experts * capacity, width)
    token_part = product("sr,sd->rd", place, partial_in.astype(jnp.bfloat16))
    both = jnp.concatenate(
        [token_part, jnp.pad(gate_part, ((0, 0), (0, 128 - gate_part.shape[1])))], axis=1
    ).astype(jnp.bfloat16)
    both, grad_in_w = lax.optimization_barrier((both, grad_in_w))
    summed = tensor_sum(both, 1)
    grad_tokens = summed[:, :width]
    grad_gate = summed[:, width : width + gate_part.shape[1]]
    grad_probs = jnp.sum(onehot * (grad_gate * live_f[:, None])[:, :, None], axis=1)
    grad_logits = (
        probs * (grad_probs - jnp.sum(probs * grad_probs, axis=1, keepdims=True))
    ).astype(jnp.bfloat16)
    grad_router = product("rd,re->de", normed_b, grad_logits)
    grad_tokens = grad_tokens + product("re,de->rd", grad_logits, router_w)
    return (grad_tokens, grad_router, grad_in_w)


def per_device(
    tokens,
    cotangent,
    expert_ids,
    image_counts,
    w_attn,
    norm_gain,
    norm_bias,
    mlp_in,
    mlp_out,
    router,
    exp_in,
    exp_out,
):
    total_rows = tokens.shape[0]
    images = total_rows // SEQ
    live = (jnp.arange(total_rows, dtype=jnp.int32) // SEQ < image_counts[0]).astype(jnp.int32)
    width_local = norm_gain.shape[2]
    heads = w_attn.shape[2] * w_attn.shape[3]
    hidden = mlp_in.shape[1]
    experts = router.shape[1]
    small = jnp.concatenate(
        [norm_gain.reshape(-1, width_local).T, norm_bias.reshape(-1, width_local).T, router], axis=1
    )
    extra = -small.shape[1] % 128
    small = jnp.pad(small, ((0, 0), (0, extra)))
    packed = jnp.concatenate(
        [
            w_attn[0].reshape(width_local, heads),
            w_attn[1].reshape(width_local, heads),
            mlp_in,
            mlp_out,
            small,
        ],
        axis=1,
    )
    whole = lax.all_gather(packed, "fsdp", axis=0, tiled=True)
    whole, exp_in, exp_out = lax.optimization_barrier((whole, exp_in, exp_out))
    in_full = lax.all_gather(exp_in, "fsdp", axis=1, tiled=True)
    out_full = lax.all_gather(exp_out, "fsdp", axis=1, tiled=True)
    attn_w = (whole[:, :heads], whole[:, heads : 2 * heads])
    up_w = whole[:, 2 * heads : 2 * heads + hidden]
    down_w = whole[:, 2 * heads + hidden : 2 * heads + 2 * hidden]
    rest = whole[:, 2 * heads + 2 * hidden :]
    gains = rest[:, :4].astype(jnp.float32).T.reshape(2, 2, -1)
    biases = rest[:, 4:8].astype(jnp.float32).T.reshape(2, 2, -1)
    router_w = rest[:, 8 : 8 + experts]

    normed, unit_a0, inverse_a0 = norm_forward(tokens, gains[0, 0], biases[0, 0])
    first_zero = normed.astype(jnp.bfloat16)
    attn_out, saved_attn_zero = attend_forward(first_zero, attn_w[0], images)
    middle_zero = tokens + attn_out
    normed, unit_c0, inverse_c0 = norm_forward(middle_zero, gains[0, 1], biases[0, 1])
    second_zero = normed.astype(jnp.bfloat16)
    dense_out, saved_dense = dense_forward(second_zero, up_w, down_w)
    after_zero = middle_zero + dense_out
    normed, unit_a1, inverse_a1 = norm_forward(after_zero, gains[1, 0], biases[1, 0])
    first_one = normed.astype(jnp.bfloat16)
    attn_out, saved_attn_one = attend_forward(first_one, attn_w[1], images)
    middle_one = after_zero + attn_out
    normed, unit_c1, inverse_c1 = norm_forward(middle_one, gains[1, 1], biases[1, 1])
    second_one = normed.astype(jnp.bfloat16)
    upstream = cotangent * live.astype(jnp.float32)[:, None]
    mixed, grad_exp_out, out_full, saved_moe = expert_forward(
        second_one, router_w, in_full, out_full, expert_ids, live, upstream
    )
    grad_second, grad_router, grad_exp_in = expert_backward(
        second_one, router_w, in_full, out_full, live, saved_moe
    )
    grad_exp_in = lax.psum_scatter(grad_exp_in, "fsdp", scatter_dimension=1, tiled=True)
    norm_delta, gain_c1, bias_c1 = norm_backward(grad_second, unit_c1, inverse_c1, gains[1, 1])
    grad_middle = upstream + norm_delta
    grad_first, grad_attn_one = attend_backward(grad_middle, first_one, attn_w[1], saved_attn_one)
    norm_delta, gain_a1, bias_a1 = norm_backward(grad_first, unit_a1, inverse_a1, gains[1, 0])
    grad_after = grad_middle + norm_delta
    grad_second_zero, grad_mlp_in, grad_mlp_out = dense_backward(
        grad_after, second_zero, up_w, down_w, saved_dense
    )
    norm_delta, gain_c0, bias_c0 = norm_backward(
        grad_second_zero, unit_c0, inverse_c0, gains[0, 1]
    )
    grad_middle_zero = grad_after + norm_delta
    grad_first_zero, grad_attn_zero = attend_backward(
        grad_middle_zero, first_zero, attn_w[0], saved_attn_zero
    )
    norm_delta, gain_a0, bias_a0 = norm_backward(
        grad_first_zero, unit_a0, inverse_a0, gains[0, 0]
    )
    grad_input = grad_middle_zero + norm_delta
    vectors = [gain_a0, gain_c0, gain_a1, gain_c1, bias_a0, bias_c0, bias_a1, bias_c1]
    small_grad = jnp.concatenate([jnp.stack(vectors, axis=1), grad_router], axis=1)
    small_grad = jnp.pad(small_grad, ((0, 0), (0, extra))).astype(jnp.bfloat16)
    packed_grad = jnp.concatenate(
        [
            grad_attn_zero,
            grad_attn_one,
            grad_mlp_in.astype(jnp.bfloat16),
            grad_mlp_out.astype(jnp.bfloat16),
            small_grad,
        ],
        axis=1,
    )
    packed_grad = with_layout_constraint(packed_grad, Layout((0, 1)))
    packed_grad, grad_exp_in, grad_exp_out, mixed = lax.optimization_barrier(
        (packed_grad, grad_exp_in, grad_exp_out, mixed)
    )
    output = middle_one + tensor_sum(mixed, 0)
    owned = lax.psum_scatter(packed_grad, "fsdp", scatter_dimension=0, tiled=True).astype(
        jnp.float32
    )
    grad_attn = jnp.stack(
        [
            owned[:, :heads].reshape(w_attn.shape[1:]),
            owned[:, heads : 2 * heads].reshape(w_attn.shape[1:]),
        ]
    )
    tail = owned[:, 2 * heads + 2 * hidden :]
    return (
        output,
        grad_input,
        grad_attn,
        tail[:, :4].T.reshape(norm_gain.shape),
        tail[:, 4:8].T.reshape(norm_bias.shape),
        owned[:, 2 * heads : 2 * heads + hidden],
        owned[:, 2 * heads + hidden : 2 * heads + 2 * hidden],
        tail[:, 8 : 8 + experts],
        grad_exp_in.astype(jnp.float32),
        grad_exp_out.astype(jnp.float32),
    )


def solution(mesh):
    in_specs = (
        P("fsdp", None),
        P("fsdp", None),
        P("fsdp", None),
        P("fsdp"),
        P(None, "fsdp", None, "tensor"),
        P(None, None, "fsdp"),
        P(None, None, "fsdp"),
        P("fsdp", "tensor"),
        P("fsdp", "tensor"),
        P("fsdp", None),
        P(None, "fsdp", "tensor"),
        P(None, "fsdp", "tensor"),
    )
    out_specs = (
        P("fsdp", None),
        P("fsdp", None),
        P(None, "fsdp", None, "tensor"),
        P(None, None, "fsdp"),
        P(None, None, "fsdp"),
        P("fsdp", "tensor"),
        P("fsdp", "tensor"),
        P("fsdp", None),
        P(None, "fsdp", "tensor"),
        P(None, "fsdp", "tensor"),
    )
    return jax.shard_map(
        per_device, mesh=mesh, in_specs=in_specs, out_specs=out_specs, check_vma=False
    )
```
